128 devices in a mesh: cube: 16 (over z, y), front: 8 (over x, core).
Axes of the slice: x: 4, y: 4, z: 4, core: 2. Of those that a mesh axis runs over, the one named last changes fastest.
Arguments:
- parent_front: float32 [16384, 16384], P('cube', 'front'), as said below
- child_entries: float32 [16384, 8192], P('cube', 'front'), as said below
- child_index: int32 [2, 64], replicated, may hold values from 0 to 127, as said below
Outputs:
- factor: float32 [16384, 16384], P('cube', 'front')
The draws below stay inside these ranges and needn't reach their ends.
Inputs may be any that keep to these rules, and one draw needn't show every extreme that they name: parent_front, taken to the front's order, is symmetric positive definite. `child_entries`: each child's contribution block is symmetric positive semidefinite. For each child s the entries child_index[s, b] are distinct parent block numbers. Within each aligned run of 8 entries of one child no two are equal modulo 16, and each remainder modulo 8 occurs exactly once in it.
All inputs are finite; a program needn't handle non-finite values.
Results may differ from the reference program's by a relative error of at most 0.000059.
Values sent between devices are 32-bit elements; how exact they have to be, the bound alone decides.
No kernel may reach another device: no remote copies, remote signals or barrier semaphores. Data moves between devices by JAX's collectives and lax.ppermute only.
A program may use at most 128 MiB of HBM per device.

```python
import math
import jax
import jax.numpy as jnp
from jax import lax

BLK = 128
RB = 8
NPB = 6
NF = 16384
CB = 8192
N_CUBE = 16
N_FRONT = 8


REACH = 3.0


def kernel_matrix(key, order_size, shift_low, shift_high):
    box_side = float(order_size) ** (1.0 / 3.0)
    key_list = jax.random.split(key, 4)
    points = jax.random.uniform(key_list[0], (order_size, 3), jnp.float32, 0.0, box_side)
    scales = jnp.exp(jax.random.uniform(key_list[1], (order_size,), jnp.float32, math.log(0.5), math.log(1.5)))
    flips = jax.random.bernoulli(key_list[2], 0.5, (order_size,))
    weights = jnp.where(flips, scales, -scales)
    diag_shift = jax.random.uniform(key_list[3], (order_size,), jnp.float32, shift_low, shift_high)
    squared = jnp.zeros((order_size, order_size), jnp.float32)
    for axis_id in range(3):
        column = points[:, axis_id]
        squared = squared + (column[:, None] - column[None, :]) ** 2
    distance = jnp.sqrt(squared)
    kernel = weights[:, None] * weights[None, :] * jnp.exp(-distance / REACH)
    same_pos = jnp.arange(order_size)[:, None] == jnp.arange(order_size)[None, :]
    return jnp.where(same_pos, kernel + diag_shift[:, None], kernel)


def draw_parent_front(key, part):
    natural = kernel_matrix(jax.random.fold_in(key, 7), NF, 1.0, 2.0)
    col_per = NF // BLK // N_FRONT
    stored = natural.reshape(RB, N_CUBE, BLK, col_per, N_FRONT, BLK).transpose(1, 0, 2, 4, 3, 5)
    return stored.reshape(NF, NF)


def draw_child_entries(key, part):
    first = kernel_matrix(jax.random.fold_in(key, 21), CB, 0.3, 1.0)
    second = kernel_matrix(jax.random.fold_in(key, 22), CB, 0.3, 1.0)
    return jnp.concatenate([first, second], axis=0)


def draw_child_index(key, part):
    groups = N_CUBE // 2
    tier_count = N_CUBE // N_FRONT
    picks = RB // N_FRONT
    results = []
    for child_id in range(2):
        child_key = jax.random.fold_in(key, 101 + child_id)
        key_list = jax.random.split(child_key, 3)
        offsets = jax.random.randint(key_list[0], (groups, N_FRONT), 0, tier_count)
        offsets = offsets.at[0].set(0)
        offsets = offsets.at[groups - 1].set(tier_count - 1)
        tiers = (offsets[:, :, None] + jnp.arange(picks, dtype=jnp.int32)[None, None, :]) % tier_count
        owners = jnp.arange(N_FRONT, dtype=jnp.int32)[None, :, None] + N_FRONT * tiers
        owners = owners.reshape(groups, RB)
        scores = jax.random.randint(key_list[1], (groups, RB), 0, 1 << 20) * RB + jnp.arange(RB, dtype=jnp.int32)[None, :]
        shuffle = jnp.argsort(scores, axis=1)
        owners = jnp.take_along_axis(owners, shuffle, axis=1)
        present = jnp.sum((owners[:, :, None] == jnp.arange(N_CUBE, dtype=jnp.int32)[None, None, :]).astype(jnp.int32), axis=1)
        before = jnp.cumsum(present, axis=0) - present
        occurrence = jnp.take_along_axis(before, owners, axis=1)
        slot_scores = jax.random.randint(key_list[2], (N_CUBE, RB), 0, 1 << 20) * RB + jnp.arange(RB, dtype=jnp.int32)[None, :]
        slot_scores = slot_scores.at[0, 0].set(-1)
        slot_scores = slot_scores.at[N_CUBE - 1, RB - 1].set(-1)
        slot_order = jnp.argsort(slot_scores, axis=1)
        slots = slot_order[owners, occurrence]
        results.append((owners + N_CUBE * slots).reshape(-1))
    return jnp.stack(results).astype(jnp.int32)


def setup_inputs(seed: int = 0) -> dict:
    keys = jax.random.split(jax.random.key(seed), 4)
    return {
        "parent_front": draw_parent_front(jax.random.fold_in(keys[3], 71), 0),
        "child_entries": draw_child_entries(jax.random.fold_in(keys[3], 71), 0),
        "child_index": draw_child_index(jax.random.fold_in(keys[3], 71), 0),
    }


EXACT = lax.Precision.HIGHEST

def reference(parent_front, child_entries, child_index):
    blocks = NF // BLK
    col_per = blocks // N_FRONT
    natural = parent_front.reshape(N_CUBE, RB, BLK, N_FRONT, col_per, BLK)
    natural = natural.transpose(1, 0, 2, 4, 3, 5).reshape(blocks, BLK, blocks, BLK)
    child_blocks = CB // BLK
    for child_id in range(2):
        entries = child_entries[child_id * CB:(child_id + 1) * CB]
        entries = entries.reshape(child_blocks, BLK, child_blocks, BLK).transpose(0, 2, 1, 3)
        target = child_index[child_id].astype(jnp.int32)
        natural = natural.at[target[:, None], :, target[None, :], :].add(entries)
    assembled = natural.reshape(NF, NF)
    pivots = NPB * BLK
    lead_factor = jnp.linalg.cholesky(assembled[:pivots, :pivots])
    panel_lower = jax.scipy.linalg.solve_triangular(lead_factor, assembled[pivots:, :pivots].T, lower=True).T
    schur_part = assembled[pivots:, pivots:] - jnp.dot(panel_lower, panel_lower.T, precision=EXACT)
    top_rows = jnp.concatenate([lead_factor, jnp.zeros((pivots, NF - pivots), jnp.float32)], axis=1)
    bottom = jnp.concatenate([panel_lower, schur_part], axis=1)
    factor = jnp.concatenate([top_rows, bottom], axis=0)
    factor = factor.reshape(RB, N_CUBE, BLK, col_per, N_FRONT, BLK).transpose(1, 0, 2, 4, 3, 5)
    return factor.reshape(NF, NF)
```

```python
import functools

import jax
import jax.numpy as jnp
from jax import lax
from jax.experimental import pallas as pl
from jax.experimental.pallas import tpu as pltpu
from jax.sharding import Mesh, PartitionSpec as P

BLK = 128
NPB = 6
NPIV = NPB * BLK
SUB = 8

EXACT = lax.Precision.HIGHEST
F32 = jnp.float32
CUBE = ("half", "res")
VMEM_LIMIT = 56 * 1024 * 1024


def find(idx_ref, base, residue):
    place = jnp.int32(0)
    for u in range(8):
        place = place + jnp.where(lax.rem(idx_ref[base + u], 8) == residue, u, 0)
    return place


def params():
    return pltpu.CompilerParams(vmem_limit_bytes=VMEM_LIMIT)


def pack_kernel(idx_ref, pos_ref, tile_ref, out_ref):
    base = pos_ref[0] * 64 + pos_ref[2] * 8
    for dest in range(8):
        col = pl.multiple_of(find(idx_ref, base, dest) * BLK, BLK)
        out_ref[dest] = tile_ref[:, pl.ds(col, BLK)]


def pack_tiles(idx, pos, child):
    def pick_row(step, idx_ref, pos_ref):
        return (find(idx_ref, pos_ref[0] * 64 + pos_ref[1] * 8, step), 0)

    return pl.pallas_call(
        pack_kernel,
        out_shape=jax.ShapeDtypeStruct((64, BLK, BLK), F32),
        grid_spec=pltpu.PrefetchScalarGridSpec(
            num_scalar_prefetch=2,
            grid=(8,),
            in_specs=[pl.BlockSpec((BLK, 8 * BLK), pick_row)],
            out_specs=pl.BlockSpec((8, BLK, BLK), lambda step, idx_ref, pos_ref: (step, 0, 0)),
        ),
        compiler_params=params(),
        name="pack_tiles",
    )(idx, pos, child)


def row_hit(idx_ref, child_id, group, residue):
    base = child_id * 64 + group * 8
    return idx_ref[base + find(idx_ref, base, residue)]


def pick_group(idx_ref, child_id, residue, wanted):
    group = jnp.int32(0)
    found = jnp.int32(0)
    for g in range(8):
        hit = row_hit(idx_ref, child_id, g, residue) == wanted
        group = group + jnp.where(hit, g, 0)
        found = found + jnp.where(hit, 1, 0)
    return group, found


def strip_kernel(idx_ref, pos_ref, parent_ref, tile_ref, out_ref):
    half, res, front = pos_ref[0], pos_ref[1], pos_ref[2]
    owns = (half == 0) & (res < NPB)
    for j in range(16):
        out_ref[j, 0] = jnp.where(owns, parent_ref[:, j * BLK:(j + 1) * BLK], 0.0)
    _, found = pick_group(idx_ref, half, res, res)

    @pl.when((found > 0) & (res < NPB))
    def _():
        for source in range(8):
            col = row_hit(idx_ref, half, source, front) // 8
            out_ref[col, 0] = out_ref[col, 0] + tile_ref[source]

    lead = out_ref[0, 0]
    for j in range(16):
        out_ref[j, 1] = lead


def make_strip(idx, pos, parent, arrived):
    def pick_tiles(step, idx_ref, pos_ref):
        return (pick_group(idx_ref, pos_ref[0], pos_ref[1], pos_ref[1])[0], 0, 0)

    return pl.pallas_call(
        strip_kernel,
        out_shape=jax.ShapeDtypeStruct((16, 2, BLK, BLK), F32),
        grid_spec=pltpu.PrefetchScalarGridSpec(
            num_scalar_prefetch=2,
            grid=(1,),
            in_specs=[
                pl.BlockSpec((BLK, 16 * BLK), lambda step, idx_ref, pos_ref: (0, 0)),
                pl.BlockSpec((8, BLK, BLK), pick_tiles),
            ],
            out_specs=pl.BlockSpec((16, 2, BLK, BLK), lambda step, idx_ref, pos_ref: (0, 0, 0, 0)),
        ),
        compiler_params=params(),
        name="make_strip",
    )(idx, pos, parent, arrived)


def spread_row(tile, j):
    return jnp.broadcast_to(tile[j:j + 1, :], (SUB, BLK))


def spread_col(tile, j):
    return jnp.broadcast_to(tile[:, j:j + 1], (SUB, BLK))


def invert_block(d_ref, b_ref):
    count = BLK // SUB
    row_id = lax.broadcasted_iota(jnp.int32, (SUB, BLK), 0)
    col_id = lax.broadcasted_iota(jnp.int32, (SUB, BLK), 1)
    for t in range(count):
        b_ref[t * SUB:(t + 1) * SUB, :] = jnp.where(col_id == row_id + t * SUB, 1.0, 0.0)
    for t in range(count):
        lead = d_ref[t * SUB:(t + 1) * SUB, :]
        side = b_ref[t * SUB:(t + 1) * SUB, :]
        cols = [spread_col(lead, t * SUB + j) for j in range(SUB)]
        entry = [[spread_row(cols[j], i) if i >= j else None for j in range(SUB)] for i in range(SUB)]
        factor = [[None] * SUB for _ in range(SUB)]
        inv = []
        for k in range(SUB):
            inv.append(1.0 / entry[k][k])
            for i in range(k + 1, SUB):
                factor[i][k] = entry[i][k] * inv[k]
            for i in range(k + 1, SUB):
                for j in range(k + 1, i + 1):
                    entry[i][j] = entry[i][j] - factor[i][k] * entry[j][k]
        rows, sides = [], []
        for j in range(SUB):
            row, extra = spread_row(lead, j), spread_row(side, j)
            for k in range(j):
                row = row - factor[j][k] * rows[k]
                extra = extra - factor[j][k] * sides[k]
            rows.append(row)
            sides.append(extra)
        done = sides[0] * (1.0 / jnp.sqrt(entry[0][0]))
        for j in range(1, SUB):
            done = jnp.where(row_id == j, sides[j] * (1.0 / jnp.sqrt(entry[j][j])), done)
        b_ref[t * SUB:(t + 1) * SUB, :] = done
        for u in range(t + 1, count):
            part = d_ref[u * SUB:(u + 1) * SUB, :]
            extra = b_ref[u * SUB:(u + 1) * SUB, :]
            raw = [spread_col(part, t * SUB + k) for k in range(SUB)]
            for k in range(SUB):
                for q in range(k):
                    raw[k] = raw[k] - factor[k][q] * raw[q]
            for k in range(SUB):
                scale = raw[k] * inv[k]
                part = part - scale * rows[k]
                extra = extra - scale * sides[k]
            d_ref[u * SUB:(u + 1) * SUB, :] = part
            b_ref[u * SUB:(u + 1) * SUB, :] = extra


def lead_kernel(pos_ref, own_ref, one_ref, two_ref, three_ref, out_ref, work_ref, d_ref, b_ref):
    chip = pos_ref[2] // 2
    for away, piece in enumerate((own_ref, one_ref, two_ref, three_ref)):
        source = lax.rem(chip + 4 - away, 4)

        @pl.when(source < 3)
        def _():
            for core in range(2):
                lane = pl.multiple_of(source * 2 * BLK + core * BLK, BLK)
                work_ref[:, pl.ds(lane, BLK)] = piece[core]

    work_ref[:, NPIV:] = jnp.zeros((NPIV, NPIV), F32)

    def eliminate(kb, carry):
        top = pl.multiple_of(kb * BLK, BLK)
        d_ref[...] = work_ref[pl.ds(top, BLK), pl.ds(top, BLK)]
        invert_block(d_ref, b_ref)
        inverse = b_ref[...]
        scaled = jnp.dot(inverse, work_ref[pl.ds(top, BLK), :], precision=EXACT)
        work_ref[pl.ds(top, BLK), :] = scaled
        work_ref[pl.ds(top, BLK), pl.ds(pl.multiple_of(NPIV + kb * BLK, BLK), BLK)] = inverse

        def reduce(i, inner):
            at = pl.multiple_of(i * BLK, BLK)
            lower = work_ref[pl.ds(top, BLK), pl.ds(at, BLK)].T
            work_ref[pl.ds(at, BLK), :] = work_ref[pl.ds(at, BLK), :] - jnp.dot(
                lower, work_ref[pl.ds(top, BLK), :], precision=EXACT)
            return inner

        lax.fori_loop(kb + 1, NPB, reduce, 0)
        return carry

    lax.fori_loop(0, NPB, eliminate, 0)
    out_ref[...] = work_ref[:, NPIV:]


def lead_inverse(pos, pieces):
    spec = pl.BlockSpec((2, NPIV, BLK), lambda step, pos_ref: (0, 0, 0))
    return pl.pallas_call(
        lead_kernel,
        out_shape=jax.ShapeDtypeStruct((NPIV, NPIV), F32),
        grid_spec=pltpu.PrefetchScalarGridSpec(
            num_scalar_prefetch=1,
            grid=(1,),
            in_specs=[spec] * 4,
            out_specs=pl.BlockSpec((NPIV, NPIV), lambda step, pos_ref: (0, 0)),
            scratch_shapes=[
                pltpu.VMEM((NPIV, 2 * NPIV), F32),
                pltpu.VMEM((BLK, BLK), F32),
                pltpu.VMEM((BLK, BLK), F32),
            ],
        ),
        compiler_params=params(),
        name="lead_inverse",
    )(pos, *pieces)


def col_panel_kernel(inverse_ref, strip_ref, high_ref, low_ref):
    strip = jnp.concatenate([strip_ref[0], strip_ref[1]], axis=1)
    panel = jnp.dot(inverse_ref[...], strip, precision=EXACT)
    high = panel.astype(jnp.bfloat16)
    high_ref[...] = high
    low_ref[...] = (panel - high.astype(F32)).astype(jnp.bfloat16)


def col_panel(inverse, strips):
    out = jax.ShapeDtypeStruct((NPIV, 16 * BLK), jnp.bfloat16)
    spec = pl.BlockSpec((NPIV, 2 * BLK), lambda step: (0, step))
    return pl.pallas_call(
        col_panel_kernel,
        out_shape=(out, out),
        grid=(8,),
        in_specs=[
            pl.BlockSpec((NPIV, NPIV), lambda step: (0, 0)),
            pl.BlockSpec((2, NPIV, BLK), lambda step: (step, 0, 0)),
        ],
        out_specs=(spec, spec),
        compiler_params=params(),
        name="col_panel",
    )(inverse, strips)


def row_panel_kernel(inverse_ref, strip_ref, out_ref):
    strip = jnp.concatenate([strip_ref[0], strip_ref[1]], axis=1)
    out_ref[...] = jnp.dot(inverse_ref[...], strip, precision=EXACT).T


def row_panel(inverse, strips):
    return pl.pallas_call(
        row_panel_kernel,
        out_shape=jax.ShapeDtypeStruct((8 * BLK, NPIV), F32),
        grid=(4,),
        in_specs=[
            pl.BlockSpec((NPIV, NPIV), lambda step: (0, 0)),
            pl.BlockSpec((2, NPIV, BLK), lambda step: (step, 0, 0)),
        ],
        out_specs=pl.BlockSpec((2 * BLK, NPIV), lambda step: (step, 0)),
        compiler_params=params(),
        name="row_panel",
    )(inverse, strips)


def finish_kernel(idx_ref, pos_ref, parent_ref, own_ref, other_ref, rows_ref, high_ref, low_ref, out_ref):
    half, res, front = pos_ref[0], pos_ref[1], pos_ref[2]
    step = pl.program_id(0)
    row_block = half * 8 + res + 16 * step
    rows = rows_ref[...]
    row_high = rows.astype(jnp.bfloat16)
    row_low = (rows - row_high.astype(F32)).astype(jnp.bfloat16)
    high = high_ref[...]
    product = jnp.dot(row_high, low_ref[...], preferred_element_type=F32)
    product = product + jnp.dot(row_low, high, preferred_element_type=F32)
    product = product + jnp.dot(row_high, high, preferred_element_type=F32)
    out_ref[...] = parent_ref[...] - product
    for child_id, tiles in ((half, own_ref), (1 - half, other_ref)):
        _, found = pick_group(idx_ref, child_id, res, row_block)

        @pl.when(found > 0)
        def _():
            for source in range(8):
                col = row_hit(idx_ref, child_id, source, front) // 8
                at = pl.ds(pl.multiple_of(col * BLK, BLK), BLK)
                out_ref[:, at] = out_ref[:, at] + tiles[source]

    @pl.when(row_block < NPB)
    def _():
        out_ref[...] = jnp.zeros_like(out_ref)

    @pl.when(front < NPB)
    def _():
        panel = rows_ref[:, pl.ds(pl.multiple_of(lax.min(front, NPB - 1) * BLK, BLK), BLK)]
        row_id = lax.broadcasted_iota(jnp.int32, (BLK, BLK), 0) + row_block * BLK
        col_id = lax.broadcasted_iota(jnp.int32, (BLK, BLK), 1) + front * BLK
        out_ref[:, :BLK] = jnp.where(row_id >= col_id, panel, 0.0)


def finish(idx, pos, parent, arrived, crossed, rows, high, low):
    def pick(step, idx_ref, pos_ref, child_id):
        row_block = pos_ref[0] * 8 + pos_ref[1] + 16 * step
        return (pick_group(idx_ref, child_id, pos_ref[1], row_block)[0], 0, 0)

    whole = pl.BlockSpec((NPIV, 16 * BLK), lambda step, idx_ref, pos_ref: (0, 0))
    return pl.pallas_call(
        finish_kernel,
        out_shape=jax.ShapeDtypeStruct((8 * BLK, 16 * BLK), F32),
        grid_spec=pltpu.PrefetchScalarGridSpec(
            num_scalar_prefetch=2,
            grid=(8,),
            in_specs=[
                pl.BlockSpec((BLK, 16 * BLK), lambda step, idx_ref, pos_ref: (step, 0)),
                pl.BlockSpec((8, BLK, BLK), lambda step, idx_ref, pos_ref: pick(step, idx_ref, pos_ref, pos_ref[0])),
                pl.BlockSpec((8, BLK, BLK), lambda step, idx_ref, pos_ref: pick(step, idx_ref, pos_ref, 1 - pos_ref[0])),
                pl.BlockSpec((BLK, NPIV), lambda step, idx_ref, pos_ref: (step, 0)),
                whole,
                whole,
            ],
            out_specs=pl.BlockSpec((BLK, 16 * BLK), lambda step, idx_ref, pos_ref: (step, 0)),
        ),
        compiler_params=params(),
        name="finish",
    )(idx, pos, parent, arrived, crossed, rows, high, low)


def body(parent_front, child_entries, child_index):
    idx = child_index.reshape(-1)
    pos = jnp.stack([lax.axis_index("half"), lax.axis_index("res"), lax.axis_index("front")]).astype(jnp.int32)
    packed = pack_tiles(idx, pos, child_entries)
    arrived = lax.all_to_all(packed, ("res", "front"), split_axis=0, concat_axis=0, tiled=True)

    strip = make_strip(idx, pos, parent_front, arrived)
    pieces = lax.all_to_all(strip, CUBE, split_axis=0, concat_axis=0, tiled=True)
    summed = pieces[:NPB] + pieces[8:8 + NPB]
    one_block = summed[:, 0].reshape(NPIV, BLK)
    lead_cols = summed[:, 1].reshape(NPIV, BLK)

    beside = lax.ppermute(lead_cols, "front", [(i, i ^ 1) for i in range(8)])
    odd = lax.axis_index("front") % 2 == 1
    pair = jnp.stack([jnp.where(odd, beside, lead_cols), jnp.where(odd, lead_cols, beside)])
    pair_parts = [pair]
    for away in range(1, 4):
        hops = [(i, (i + 2 * away) % 8) for i in range(6)]
        pair_parts.append(lax.ppermute(pair, "front", hops))

    strips = lax.all_gather(one_block, CUBE, axis=0, tiled=False)
    moved = lax.ppermute(one_block, ("half", "res", "front"),
                         [(c + 16 * f, c * 8 + f) for c in range(16) for f in range(8)])
    row_strips = lax.all_gather(moved, "front", axis=0, tiled=False)
    crossed = lax.ppermute(arrived, "half", [(0, 1), (1, 0)])

    inverse = lead_inverse(pos, pair_parts)
    high, low = col_panel(inverse, strips)
    rows = row_panel(inverse, row_strips)
    return finish(idx, pos, parent_front, arrived, crossed, rows, high, low)


def solution(mesh):
    split = Mesh(mesh.devices.reshape(2, 8, 8), ("half", "res", "front"))
    placed = P(CUBE, "front")
    return jax.shard_map(
        body, mesh=split, in_specs=(placed, placed, P()), out_specs=placed, check_vma=False
    )
```

```python
import jax
import jax.numpy as jnp
from jax import lax
from jax.experimental import pallas as pl
from jax.experimental.pallas import tpu as pltpu
from jax.sharding import Mesh, PartitionSpec as P


BLK = 128
NPB = 6
NPIV = NPB * BLK
SUB = 8

EXACT = lax.Precision.HIGHEST
F32 = jnp.float32
CUBE = ("zh", "zl", "y")
FRONT = ("x", "core")
VMEM_LIMIT = 56 * 1024 * 1024


GROUP = 0
COLUMN = 16
ROW_PICK = 32
COL_PICK = 40
PIVOT = 48
HALF, RES, FRONT_AT = 50, 51, 52
SPARE = 53
TABLE = 64


def params():
    return pltpu.CompilerParams(vmem_limit_bytes=VMEM_LIMIT)


def table_kernel(pos_ref, idx_ref, tab_ref):
    half, res, front = pos_ref[0], pos_ref[1], pos_ref[2]
    for at in range(TABLE):
        tab_ref[at] = jnp.int32(-1)
    tab_ref[HALF], tab_ref[RES], tab_ref[FRONT_AT] = half, res, front
    for child_id in range(2):
        for run in range(8):
            row, col = jnp.int32(0), jnp.int32(0)
            for u in range(8):
                entry = idx_ref[child_id, run * 8 + u]
                residue = entry & 7
                row = jnp.where(residue == res, entry, row)
                col = jnp.where(residue == front, entry, col)
            mine = ((row >> 3) & 1) == half
            tab_ref[jnp.where(mine, GROUP + child_id * 8 + (row >> 4), SPARE)] = jnp.int32(run)
            tab_ref[jnp.where(row == res, PIVOT + child_id, SPARE)] = jnp.int32(run)
            tab_ref[COLUMN + child_id * 8 + run] = col >> 3
    for u in range(8):
        tab_ref[ROW_PICK + (idx_ref[half, res * 8 + u] & 7)] = jnp.int32(u)
        tab_ref[COL_PICK + (idx_ref[half, front * 8 + u] & 7)] = jnp.int32(u)


def make_table(pos, idx):
    smem = pl.BlockSpec(memory_space=pltpu.SMEM)
    return pl.pallas_call(
        table_kernel,
        out_shape=jax.ShapeDtypeStruct((TABLE,), jnp.int32),
        in_specs=[smem, smem],
        out_specs=smem,
        name="make_table",
    )(pos, idx)


def pack_kernel(tab_ref, tile_ref, out_ref):
    for dest in range(8):
        col = pl.multiple_of(tab_ref[COL_PICK + dest] * BLK, BLK)
        out_ref[dest] = tile_ref[:, pl.ds(col, BLK)]


def pack_tiles(tab, child):
    return pl.pallas_call(
        pack_kernel,
        out_shape=jax.ShapeDtypeStruct((64, BLK, BLK), F32),
        grid_spec=pltpu.PrefetchScalarGridSpec(
            num_scalar_prefetch=1,
            grid=(8,),
            in_specs=[pl.BlockSpec((BLK, 8 * BLK), lambda step, tab_ref: (tab_ref[ROW_PICK + step], 0))],
            out_specs=pl.BlockSpec((8, BLK, BLK), lambda step, tab_ref: (step, 0, 0)),
        ),
        compiler_params=params(),
        name="pack_tiles",
    )(tab, child)


def strip_kernel(tab_ref, parent_ref, tile_ref, out_ref):
    half, res = tab_ref[HALF], tab_ref[RES]
    owns = (half == 0) & (res < NPB)

    @pl.when(owns)
    def _():
        for j in range(16):
            out_ref[j, 0] = parent_ref[:, j * BLK:(j + 1) * BLK]

    @pl.when(jnp.logical_not(owns))
    def _():
        for j in range(16):
            out_ref[j, 0] = jnp.zeros((BLK, BLK), F32)

    @pl.when((tab_ref[PIVOT + half] >= 0) & (res < NPB))
    def _():
        for source in range(8):
            col = tab_ref[COLUMN + half * 8 + source]
            out_ref[col, 0] = out_ref[col, 0] + tile_ref[source]

    lead = out_ref[0, 0]
    for j in range(16):
        out_ref[j, 1] = lead


def make_strip(tab, parent, arrived):
    def pick_tiles(step, tab_ref):
        return (lax.max(tab_ref[PIVOT + tab_ref[HALF]], 0), 0, 0)

    return pl.pallas_call(
        strip_kernel,
        out_shape=jax.ShapeDtypeStruct((16, 2, BLK, BLK), F32),
        grid_spec=pltpu.PrefetchScalarGridSpec(
            num_scalar_prefetch=1,
            grid=(1,),
            in_specs=[
                pl.BlockSpec((BLK, 16 * BLK), lambda step, tab_ref: (0, 0)),
                pl.BlockSpec((8, BLK, BLK), pick_tiles),
            ],
            out_specs=pl.BlockSpec((16, 2, BLK, BLK), lambda step, tab_ref: (0, 0, 0, 0)),
        ),
        compiler_params=params(),
        name="make_strip",
    )(tab, parent, arrived)


def spread_row(tile, j):
    return jnp.broadcast_to(tile[j:j + 1, :], (SUB, BLK))


def spread_col(tile, j):
    return jnp.broadcast_to(tile[:, j:j + 1], (SUB, BLK))


def invert_block(d_ref, b_ref):
    count = BLK // SUB
    row_id = lax.broadcasted_iota(jnp.int32, (SUB, BLK), 0)
    col_id = lax.broadcasted_iota(jnp.int32, (SUB, BLK), 1)
    for t in range(count):
        b_ref[t * SUB:(t + 1) * SUB, :] = jnp.where(col_id == row_id + t * SUB, 1.0, 0.0)
    for t in range(count):
        lead = d_ref[t * SUB:(t + 1) * SUB, :]
        side = b_ref[t * SUB:(t + 1) * SUB, :]
        cols = [spread_col(lead, t * SUB + j) for j in range(SUB)]
        entry = [[spread_row(cols[j], i) if i >= j else None for j in range(SUB)] for i in range(SUB)]
        factor = [[None] * SUB for _ in range(SUB)]
        inv = []
        for k in range(SUB):
            inv.append(1.0 / entry[k][k])
            for i in range(k + 1, SUB):
                factor[i][k] = entry[i][k] * inv[k]
            for i in range(k + 1, SUB):
                for j in range(k + 1, i + 1):
                    entry[i][j] = entry[i][j] - factor[i][k] * entry[j][k]
        rows, sides = [], []
        for j in range(SUB):
            row, extra = spread_row(lead, j), spread_row(side, j)
            for k in range(j):
                row = row - factor[j][k] * rows[k]
                extra = extra - factor[j][k] * sides[k]
            rows.append(row)
            sides.append(extra)
        done = sides[0] * (1.0 / jnp.sqrt(entry[0][0]))
        for j in range(1, SUB):
            done = jnp.where(row_id == j, sides[j] * (1.0 / jnp.sqrt(entry[j][j])), done)
        b_ref[t * SUB:(t + 1) * SUB, :] = done
        for u in range(t + 1, count):
            part = d_ref[u * SUB:(u + 1) * SUB, :]
            extra = b_ref[u * SUB:(u + 1) * SUB, :]
            raw = [spread_col(part, t * SUB + k) for k in range(SUB)]
            for k in range(SUB):
                for q in range(k):
                    raw[k] = raw[k] - factor[k][q] * raw[q]
            for k in range(SUB):
                scale = raw[k] * inv[k]
                part = part - scale * rows[k]
                extra = extra - scale * sides[k]
            d_ref[u * SUB:(u + 1) * SUB, :] = part
            b_ref[u * SUB:(u + 1) * SUB, :] = extra


def lead_kernel(tab_ref, *refs):
    pieces, (out_ref, work_ref, d_ref, b_ref) = refs[:8], refs[8:]
    chip, core = tab_ref[FRONT_AT] // 2, lax.rem(tab_ref[FRONT_AT], 2)
    for away in range(4):
        source = lax.rem(chip + 4 - away, 4)

        @pl.when(source < 3)
        def _():
            for other in range(2):
                lane = (source * 2 + lax.rem(core + other, 2)) * BLK
                work_ref[:, pl.ds(pl.multiple_of(lane, BLK), BLK)] = pieces[4 * other + away][...]

    for i in range(NPB):
        rows = slice(i * BLK, (i + 1) * BLK)
        row_id = lax.broadcasted_iota(jnp.int32, (BLK, NPIV), 0) + i * BLK
        col_id = lax.broadcasted_iota(jnp.int32, (BLK, NPIV), 1)
        work_ref[rows, NPIV:] = jnp.where(row_id == col_id, 1.0, 0.0)

    def eliminate(kb, carry):
        top = pl.ds(pl.multiple_of(kb * BLK, BLK), BLK)
        window = pl.ds(pl.multiple_of((kb + 1) * BLK, BLK), NPIV)
        d_ref[...] = work_ref[top, top]
        invert_block(d_ref, b_ref)
        work_ref[top, window] = jnp.dot(b_ref[...], work_ref[top, window], precision=EXACT)
        for k in range(NPB - 1):

            @pl.when(kb == k)
            def _():
                pivot = slice(k * BLK, (k + 1) * BLK)
                below = slice((k + 1) * BLK, NPIV)
                wide = slice((k + 1) * BLK, (k + 1) * BLK + NPIV)
                lower = work_ref[pivot, below].T
                work_ref[below, wide] = work_ref[below, wide] - jnp.dot(
                    lower, work_ref[pivot, wide], precision=EXACT)

        return carry

    lax.fori_loop(0, NPB, eliminate, 0)
    out_ref[...] = work_ref[:, NPIV:]


def lead_inverse(tab, pieces):
    return pl.pallas_call(
        lead_kernel,
        out_shape=jax.ShapeDtypeStruct((NPIV, NPIV), F32),
        grid_spec=pltpu.PrefetchScalarGridSpec(
            num_scalar_prefetch=1,
            grid=(1,),
            in_specs=[pl.BlockSpec((NPIV, BLK), lambda step, tab_ref: (0, 0))] * 8,
            out_specs=pl.BlockSpec((NPIV, NPIV), lambda step, tab_ref: (0, 0)),
            scratch_shapes=[
                pltpu.VMEM((NPIV, 2 * NPIV), F32),
                pltpu.VMEM((BLK, BLK), F32),
                pltpu.VMEM((BLK, BLK), F32),
            ],
        ),
        compiler_params=params(),
        name="lead_inverse",
    )(tab, *pieces)


def halves(value):
    high = value.astype(jnp.bfloat16)
    return high, (value - high.astype(F32)).astype(jnp.bfloat16)


def dot_halves(left, right):
    product = jnp.dot(left[0], right[1], preferred_element_type=F32)
    product = product + jnp.dot(left[1], right[0], preferred_element_type=F32)
    return product + jnp.dot(left[0], right[0], preferred_element_type=F32)


def whole(*shape):
    return pl.BlockSpec(shape, lambda step, tab_ref: (0,) * len(shape))


def col_kernel(inverse_ref, strip_ref, out_ref):
    inverse = halves(inverse_ref[...])
    strip = jnp.concatenate([strip_ref[0], strip_ref[1], strip_ref[2], strip_ref[3]], axis=1)
    high, low = halves(dot_halves(inverse, halves(strip)))
    out_ref[:NPIV, :] = low
    out_ref[NPIV:, :] = high


def col_panel(inverse, piece):
    return pl.pallas_call(
        col_kernel,
        out_shape=jax.ShapeDtypeStruct((2 * NPIV, 4 * BLK), jnp.bfloat16),
        compiler_params=params(),
        name="col_panel",
    )(inverse, piece)


def row_kernel(tab_ref, inverse_ref, *refs):
    row_refs, rows_ref = refs[:8], refs[8]
    chip, core = tab_ref[FRONT_AT] // 2, lax.rem(tab_ref[FRONT_AT], 2)
    inverse = halves(inverse_ref[...])
    for away in range(4):
        strip = jnp.concatenate([row_refs[away][...], row_refs[4 + away][...]], axis=1)
        panel = dot_halves(inverse, halves(strip)).T
        pair = lax.rem(chip + 8 - away - tab_ref[RES] // 2, 4)
        for other in range(2):
            at = (pair * 2 + lax.rem(core + other, 2)) * BLK
            rows_ref[pl.ds(pl.multiple_of(at, BLK), BLK), :] = panel[other * BLK:(other + 1) * BLK]


def row_panel(tab, inverse, pieces):
    return pl.pallas_call(
        row_kernel,
        out_shape=jax.ShapeDtypeStruct((8 * BLK, NPIV), F32),
        grid_spec=pltpu.PrefetchScalarGridSpec(
            num_scalar_prefetch=1,
            grid=(1,),
            in_specs=[whole(NPIV, NPIV)] + [whole(NPIV, BLK)] * 8,
            out_specs=whole(8 * BLK, NPIV),
        ),
        compiler_params=params(),
        name="row_panel",
    )(tab, inverse, *pieces)


def slot_col(tab_ref, slot):
    z = tab_ref[HALF] * 2 + tab_ref[RES] // 4
    y = lax.rem(tab_ref[RES], 4)
    return lax.rem(z + 4 - slot % 4, 4) * 4 + lax.rem(y + 4 - slot // 4, 4)


def finish_kernel(tab_ref, parent_ref, own0, own1, other0, other1, rows_ref, *refs):
    col_refs, out_ref = refs[:4], refs[4]
    half, res, front = tab_ref[HALF], tab_ref[RES], tab_ref[FRONT_AT]
    step = pl.program_id(0)
    high, low = halves(rows_ref[...])
    both = jnp.concatenate([high, low], axis=1)
    for away in range(4):
        product = jnp.dot(both, col_refs[away][...], preferred_element_type=F32)
        product = product + jnp.dot(high, col_refs[away][NPIV:, :], preferred_element_type=F32)
        for part in range(4):
            at = pl.ds(pl.multiple_of(slot_col(tab_ref, 4 * away + part) * BLK, BLK), BLK)
            out_ref[:, at] = parent_ref[:, at] - product[:, part * BLK:(part + 1) * BLK]
    for part, tile_refs in enumerate(((own0, other0), (own1, other1))):
        row_block = half * 8 + res + 16 * (2 * step + part)
        rows = slice(part * BLK, (part + 1) * BLK)
        for child_id, tiles in ((half, tile_refs[0]), (1 - half, tile_refs[1])):
            group = tab_ref[GROUP + child_id * 8 + 2 * step + part]

            @pl.when(group >= 0)
            def _():
                for source in range(8):
                    col = tab_ref[COLUMN + child_id * 8 + source]
                    at = pl.ds(pl.multiple_of(col * BLK, BLK), BLK)
                    out_ref[rows, at] = out_ref[rows, at] + tiles[source]

        @pl.when(row_block < NPB)
        def _():
            out_ref[rows, :] = jnp.zeros((BLK, 16 * BLK), F32)

        @pl.when(front < NPB)
        def _():
            lane = pl.multiple_of(lax.min(front, NPB - 1) * BLK, BLK)
            row_id = lax.broadcasted_iota(jnp.int32, (BLK, BLK), 0) + row_block * BLK
            col_id = lax.broadcasted_iota(jnp.int32, (BLK, BLK), 1) + front * BLK
            out_ref[rows, :BLK] = jnp.where(row_id >= col_id, rows_ref[rows, pl.ds(lane, BLK)], 0.0)


def finish(tab, parent, arrived, crossed, rows, cols):
    def tiles(own, part):
        def pick(step, tab_ref):
            child_id = tab_ref[HALF] if own else 1 - tab_ref[HALF]
            return (lax.max(tab_ref[GROUP + child_id * 8 + 2 * step + part], 0), 0, 0)

        return pl.BlockSpec((8, BLK, BLK), pick)

    wide = pl.BlockSpec((2 * NPIV, 4 * BLK), lambda step, tab_ref: (0, 0))
    mine = lambda width: pl.BlockSpec((2 * BLK, width), lambda step, tab_ref: (step, 0))
    return pl.pallas_call(
        finish_kernel,
        out_shape=jax.ShapeDtypeStruct((8 * BLK, 16 * BLK), F32),
        grid_spec=pltpu.PrefetchScalarGridSpec(
            num_scalar_prefetch=1,
            grid=(4,),
            in_specs=[mine(16 * BLK), tiles(True, 0), tiles(True, 1), tiles(False, 0), tiles(False, 1),
                      mine(NPIV)] + [wide] * 4,
            out_specs=mine(16 * BLK),
        ),
        compiler_params=params(),
        name="finish",
    )(tab, parent, arrived, arrived, crossed, crossed, rows, *cols)


def shift(value, axis, size, away):
    return lax.ppermute(value, axis, [(i, (i + away) % size) for i in range(size)])


def gather_front(block, sources=4):
    near = [block]
    for away in range(1, 4):
        near.append(lax.ppermute(block, "x", [(i, (i + away) % 4) for i in range(sources)]))
    return near + [shift(piece, "core", 2, 1) for piece in near]


def row_routes():
    routes = []
    for c in range(16):
        for i in range(8):
            chip = (i // 2 + (c % 8) // 2) % 4
            routes.append((c + 16 * i, c * 8 + chip * 2 + i % 2))
    return routes


def staged(parent_front, child_entries, child_index):
    half, front = lax.axis_index("zh"), lax.axis_index("x") * 2 + lax.axis_index("core")
    pos = jnp.stack([half, lax.axis_index("zl") * 4 + lax.axis_index("y"), front]).astype(jnp.int32)
    tab = make_table(pos, child_index)
    packed = pack_tiles(tab, child_entries)
    arrived = lax.all_to_all(packed, ("zl", "y", "x", "core"), split_axis=0, concat_axis=0, tiled=True)

    strip = make_strip(tab, parent_front, arrived)
    pieces = lax.all_to_all(strip, CUBE, split_axis=0, concat_axis=0, tiled=True)
    summed = pieces[:NPB] + pieces[8:8 + NPB]
    one_block = summed[:, 0].reshape(NPIV, BLK)
    lead_cols = summed[:, 1].reshape(NPIV, BLK)

    along_z = [one_block] + [shift(one_block, ("zh", "zl"), 4, away) for away in range(1, 4)]
    lead_pieces = gather_front(lead_cols, 3)
    moved = lax.ppermute(one_block, CUBE + FRONT, row_routes())
    along_z = jnp.stack(along_z)
    col_pieces = [along_z]
    for away in range(1, 4):
        col_pieces.append(shift(along_z, "y", 4, away))
    row_pieces = gather_front(moved)
    crossed = shift(arrived, "zh", 2, 1)

    inverse = lead_inverse(tab, lead_pieces)
    cols = []
    for away in range(4):
        cols.append(col_panel(inverse, col_pieces[away]))
    rows = row_panel(tab, inverse, row_pieces)
    return finish(tab, parent_front, arrived, crossed, rows, cols)


def solution(mesh):
    split = Mesh(mesh.devices.reshape(2, 2, 4, 4, 2), CUBE + FRONT)
    placed = P(CUBE, FRONT)
    return jax.shard_map(
        staged, mesh=split, in_specs=(placed, placed, P()), out_specs=placed, check_vma=False
    )
```

```python
import jax
import jax.numpy as jnp
from jax import lax
from jax.experimental import pallas as pl
from jax.experimental.pallas import tpu as pltpu
from jax.sharding import Mesh, PartitionSpec as P


BLK = 128
NPB = 6
NPIV = NPB * BLK
SUB = 8

EXACT = lax.Precision.HIGHEST
F32 = jnp.float32
CUBE = ("zh", "zl", "y")
FRONT = ("x", "core")
VMEM_LIMIT = 56 * 1024 * 1024


GROUP = 0
COLUMN = 16
ROW_PICK = 32
COL_PICK = 40
PIVOT = 48
HALF, RES, FRONT_AT = 50, 51, 52
CROSS = 53
CROSSINGS = 61
SPARE = 62
TABLE = 64


def params():
    return pltpu.CompilerParams(vmem_limit_bytes=VMEM_LIMIT)


def table_kernel(pos_ref, idx_ref, tab_ref):
    half, res, front = pos_ref[0], pos_ref[1], pos_ref[2]
    for at in range(TABLE):
        tab_ref[at] = jnp.int32(-1)
    tab_ref[HALF], tab_ref[RES], tab_ref[FRONT_AT] = half, res, front
    for child_id in range(2):
        for run in range(8):
            row, col = jnp.int32(0), jnp.int32(0)
            for u in range(8):
                entry = idx_ref[child_id, run * 8 + u]
                residue = entry & 7
                row = jnp.where(residue == res, entry, row)
                col = jnp.where(residue == front, entry, col)
            mine = ((row >> 3) & 1) == half
            tab_ref[jnp.where(mine, GROUP + child_id * 8 + (row >> 4), SPARE)] = jnp.int32(run)
            tab_ref[jnp.where(row == res, PIVOT + child_id, SPARE)] = jnp.int32(run)
            tab_ref[COLUMN + child_id * 8 + run] = col >> 3
    count = jnp.int32(0)
    last = jnp.int32(0)
    for i in range(8):
        hit = tab_ref[GROUP + (1 - half) * 8 + i] >= 0
        tab_ref[jnp.where(hit, CROSS + count, SPARE)] = jnp.int32(i)
        last = jnp.where(hit, i, last)
        count = count + jnp.where(hit, 1, 0)
    for i in range(8):
        tab_ref[CROSS + i] = jnp.where(i < count, tab_ref[CROSS + i], last)
    tab_ref[CROSSINGS] = count
    for u in range(8):
        tab_ref[ROW_PICK + (idx_ref[half, res * 8 + u] & 7)] = jnp.int32(u)
        tab_ref[COL_PICK + (idx_ref[half, front * 8 + u] & 7)] = jnp.int32(u)


def make_table(pos, idx):
    smem = pl.BlockSpec(memory_space=pltpu.SMEM)
    return pl.pallas_call(
        table_kernel,
        out_shape=jax.ShapeDtypeStruct((TABLE,), jnp.int32),
        in_specs=[smem, smem],
        out_specs=smem,
        name="make_table",
    )(pos, idx)


def pack_kernel(tab_ref, even_ref, odd_ref, out_ref):
    for dest in range(8):
        col = pl.multiple_of(tab_ref[COL_PICK + dest] * BLK, BLK)
        out_ref[dest] = even_ref[:, pl.ds(col, BLK)]
        out_ref[8 + dest] = odd_ref[:, pl.ds(col, BLK)]


def pack_tiles(tab, child):
    return pl.pallas_call(
        pack_kernel,
        out_shape=jax.ShapeDtypeStruct((64, BLK, BLK), F32),
        grid_spec=pltpu.PrefetchScalarGridSpec(
            num_scalar_prefetch=1,
            grid=(4,),
            in_specs=[
                pl.BlockSpec((BLK, 8 * BLK), lambda step, tab_ref: (tab_ref[ROW_PICK + 2 * step], 0)),
                pl.BlockSpec((BLK, 8 * BLK), lambda step, tab_ref: (tab_ref[ROW_PICK + 2 * step + 1], 0)),
            ],
            out_specs=pl.BlockSpec((16, BLK, BLK), lambda step, tab_ref: (step, 0, 0)),
        ),
        compiler_params=params(),
        name="pack_tiles",
    )(tab, child, child)


def strip_kernel(tab_ref, parent_ref, tile_ref, out_ref):
    half, res = tab_ref[HALF], tab_ref[RES]
    owns = (half == 0) & (res < NPB)

    @pl.when(owns)
    def _():
        for j in range(16):
            out_ref[j, 0] = parent_ref[:, j * BLK:(j + 1) * BLK]

    @pl.when(jnp.logical_not(owns))
    def _():
        for j in range(16):
            out_ref[j, 0] = jnp.zeros((BLK, BLK), F32)

    @pl.when((tab_ref[PIVOT + half] >= 0) & (res < NPB))
    def _():
        for source in range(8):
            col = tab_ref[COLUMN + half * 8 + source]
            out_ref[col, 0] = out_ref[col, 0] + tile_ref[source]

    lead = out_ref[0, 0]
    for j in range(16):
        out_ref[j, 1] = lead


def make_strip(tab, parent, arrived):
    def pick_tiles(step, tab_ref):
        return (lax.max(tab_ref[PIVOT + tab_ref[HALF]], 0), 0, 0)

    return pl.pallas_call(
        strip_kernel,
        out_shape=jax.ShapeDtypeStruct((16, 2, BLK, BLK), F32),
        grid_spec=pltpu.PrefetchScalarGridSpec(
            num_scalar_prefetch=1,
            grid=(1,),
            in_specs=[
                pl.BlockSpec((BLK, 16 * BLK), lambda step, tab_ref: (0, 0)),
                pl.BlockSpec((8, BLK, BLK), pick_tiles),
            ],
            out_specs=pl.BlockSpec((16, 2, BLK, BLK), lambda step, tab_ref: (0, 0, 0, 0)),
        ),
        compiler_params=params(),
        name="make_strip",
    )(tab, parent, arrived)


def spread_row(tile, j):
    return jnp.broadcast_to(tile[j:j + 1, :], (SUB, BLK))


def spread_col(tile, j):
    return jnp.broadcast_to(tile[:, j:j + 1], (SUB, BLK))


def invert_block(d_ref, b_ref):
    count = BLK // SUB
    row_id = lax.broadcasted_iota(jnp.int32, (SUB, BLK), 0)
    col_id = lax.broadcasted_iota(jnp.int32, (SUB, BLK), 1)
    for t in range(count):
        b_ref[t * SUB:(t + 1) * SUB, :] = jnp.where(col_id == row_id + t * SUB, 1.0, 0.0)
    for t in range(count):
        lead = d_ref[t * SUB:(t + 1) * SUB, :]
        side = b_ref[t * SUB:(t + 1) * SUB, :]
        cols = [spread_col(lead, t * SUB + j) for j in range(SUB)]
        entry = [[spread_row(cols[j], i) if i >= j else None for j in range(SUB)] for i in range(SUB)]
        factor = [[None] * SUB for _ in range(SUB)]
        inv = []
        for k in range(SUB):
            inv.append(1.0 / entry[k][k])
            for i in range(k + 1, SUB):
                factor[i][k] = entry[i][k] * inv[k]
            for i in range(k + 1, SUB):
                for j in range(k + 1, i + 1):
                    entry[i][j] = entry[i][j] - factor[i][k] * entry[j][k]
        rows, sides = [], []
        for j in range(SUB):
            row, extra = spread_row(lead, j), spread_row(side, j)
            for k in range(j):
                row = row - factor[j][k] * rows[k]
                extra = extra - factor[j][k] * sides[k]
            rows.append(row)
            sides.append(extra)
        done = sides[0] * (1.0 / jnp.sqrt(entry[0][0]))
        for j in range(1, SUB):
            done = jnp.where(row_id == j, sides[j] * (1.0 / jnp.sqrt(entry[j][j])), done)
        b_ref[t * SUB:(t + 1) * SUB, :] = done
        for u in range(t + 1, count):
            part = d_ref[u * SUB:(u + 1) * SUB, :]
            extra = b_ref[u * SUB:(u + 1) * SUB, :]
            raw = [spread_col(part, t * SUB + k) for k in range(SUB)]
            for k in range(SUB):
                for q in range(k):
                    raw[k] = raw[k] - factor[k][q] * raw[q]
            for k in range(SUB):
                scale = raw[k] * inv[k]
                part = part - scale * rows[k]
                extra = extra - scale * sides[k]
            d_ref[u * SUB:(u + 1) * SUB, :] = part
            b_ref[u * SUB:(u + 1) * SUB, :] = extra


def lead_kernel(tab_ref, *refs):
    pieces, (high_ref, low_ref, work_ref, d_ref, b_ref) = refs[:8], refs[8:]
    chip, core = tab_ref[FRONT_AT] // 2, lax.rem(tab_ref[FRONT_AT], 2)
    for away in range(4):
        source = lax.rem(chip + 4 - away, 4)

        @pl.when(source < 3)
        def _():
            for other in range(2):
                lane = (source * 2 + lax.rem(core + other, 2)) * BLK
                work_ref[:, pl.ds(pl.multiple_of(lane, BLK), BLK)] = pieces[4 * other + away][...]

    for i in range(NPB):
        rows = slice(i * BLK, (i + 1) * BLK)
        row_id = lax.broadcasted_iota(jnp.int32, (BLK, NPIV), 0) + i * BLK
        col_id = lax.broadcasted_iota(jnp.int32, (BLK, NPIV), 1)
        work_ref[rows, NPIV:] = jnp.where(row_id == col_id, 1.0, 0.0)

    def eliminate(kb, carry):
        top = pl.ds(pl.multiple_of(kb * BLK, BLK), BLK)
        window = pl.ds(pl.multiple_of((kb + 1) * BLK, BLK), NPIV)
        d_ref[...] = work_ref[top, top]
        invert_block(d_ref, b_ref)
        work_ref[top, window] = jnp.dot(b_ref[...], work_ref[top, window], precision=EXACT)
        for k in range(NPB - 1):

            @pl.when(kb == k)
            def _():
                pivot = slice(k * BLK, (k + 1) * BLK)
                below = slice((k + 1) * BLK, NPIV)
                wide = slice((k + 1) * BLK, (k + 1) * BLK + NPIV)
                lower = work_ref[pivot, below].T
                work_ref[below, wide] = work_ref[below, wide] - jnp.dot(
                    lower, work_ref[pivot, wide], precision=EXACT)

        return carry

    lax.fori_loop(0, NPB, eliminate, 0)
    inverse = work_ref[:, NPIV:]
    high, low = halves(inverse)
    high_ref[...] = high
    low_ref[...] = low


def lead_inverse(tab, pieces):
    return pl.pallas_call(
        lead_kernel,
        out_shape=(jax.ShapeDtypeStruct((NPIV, NPIV), jnp.bfloat16),) * 2,
        grid_spec=pltpu.PrefetchScalarGridSpec(
            num_scalar_prefetch=1,
            grid=(1,),
            in_specs=[pl.BlockSpec((NPIV, BLK), lambda step, tab_ref: (0, 0))] * 8,
            out_specs=(pl.BlockSpec((NPIV, NPIV), lambda step, tab_ref: (0, 0)),) * 2,
            scratch_shapes=[
                pltpu.VMEM((NPIV, 2 * NPIV), F32),
                pltpu.VMEM((BLK, BLK), F32),
                pltpu.VMEM((BLK, BLK), F32),
            ],
        ),
        compiler_params=params(),
        name="lead_inverse",
    )(tab, *pieces)


def halves(value):
    high = value.astype(jnp.bfloat16)
    return high, (value - high.astype(F32)).astype(jnp.bfloat16)


def dot_halves(left, right):
    product = jnp.dot(left[0], right[1], preferred_element_type=F32)
    product = product + jnp.dot(left[1], right[0], preferred_element_type=F32)
    return product + jnp.dot(left[0], right[0], preferred_element_type=F32)


def lower_dot(left, right):
    step = 2 * BLK
    bands = []
    for at in range(0, NPIV, step):
        rows, cols = slice(at, at + step), slice(0, at + step)
        bands.append(dot_halves([part[rows, cols] for part in left], [part[cols] for part in right]))
    return jnp.concatenate(bands, axis=0)


def whole(*shape):
    return pl.BlockSpec(shape, lambda step, tab_ref: (0,) * len(shape))


def col_kernel(high_in, low_in, *refs):
    strip_refs, out_ref = refs[:-1], refs[-1]
    inverse = high_in[...], low_in[...]
    blocks = []
    for ref in strip_refs:
        blocks += [ref[...]] if ref.shape == (NPIV, BLK) else [ref[part] for part in range(ref.shape[0])]
    high, low = halves(lower_dot(inverse, halves(jnp.concatenate(blocks, axis=1))))
    out_ref[:NPIV, :] = low
    out_ref[NPIV:, :] = high


def col_panel(inverse, pieces):
    count = sum(piece.size for piece in pieces) // (NPIV * BLK)
    return pl.pallas_call(
        col_kernel,
        out_shape=jax.ShapeDtypeStruct((2 * NPIV, count * BLK), jnp.bfloat16),
        compiler_params=params(),
        name="col_panel",
    )(*inverse, *pieces)


def row_kernel(tab_ref, high_in, low_in, *refs):
    row_refs, rows_ref = refs[:8], refs[8]
    chip, core = tab_ref[FRONT_AT] // 2, lax.rem(tab_ref[FRONT_AT], 2)
    inverse = high_in[...], low_in[...]
    for away in range(4):
        strip = jnp.concatenate([row_refs[away][...], row_refs[4 + away][...]], axis=1)
        panel = lower_dot(inverse, halves(strip)).T
        pair = lax.rem(chip + 8 - away - tab_ref[RES] // 2, 4)
        for other in range(2):
            at = (pair * 2 + lax.rem(core + other, 2)) * BLK
            rows_ref[pl.ds(pl.multiple_of(at, BLK), BLK), :] = panel[other * BLK:(other + 1) * BLK]


def row_panel(tab, inverse, pieces):
    return pl.pallas_call(
        row_kernel,
        out_shape=jax.ShapeDtypeStruct((8 * BLK, NPIV), F32),
        grid_spec=pltpu.PrefetchScalarGridSpec(
            num_scalar_prefetch=1,
            grid=(1,),
            in_specs=[whole(NPIV, NPIV)] * 2 + [whole(NPIV, BLK)] * 8,
            out_specs=whole(8 * BLK, NPIV),
        ),
        compiler_params=params(),
        name="row_panel",
    )(tab, *inverse, *pieces)


SLOTS = [
    [(0, away) for away in range(4)] + [(deep, 0) for deep in range(1, 4)],
    [(deep, away) for away in (1, 3) for deep in range(1, 4)],
    [(deep, 2) for deep in range(1, 4)],
]


def slot_col(tab_ref, deep, away):
    z = tab_ref[HALF] * 2 + (tab_ref[RES] >> 2)
    y = tab_ref[RES] & 3
    return ((z + 4 - deep) & 3) * 4 + ((y + 4 - away) & 3)


def finish_kernel(tab_ref, parent_ref, own0, own1, rows_ref, *refs):
    col_refs, out_ref = refs[:-1], refs[-1]
    half, res, front = tab_ref[HALF], tab_ref[RES], tab_ref[FRONT_AT]
    step = pl.program_id(0)
    high, low = halves(rows_ref[...])
    both = jnp.concatenate([high, low], axis=1)
    for slots, ref in zip(SLOTS, col_refs):
        product = jnp.dot(both, ref[...], preferred_element_type=F32)
        product = product + jnp.dot(high, ref[NPIV:, :], preferred_element_type=F32)
        for part, place in enumerate(slots):
            at = pl.ds(pl.multiple_of(slot_col(tab_ref, *place) * BLK, BLK), BLK)
            out_ref[:, at] = parent_ref[:, at] - product[:, part * BLK:(part + 1) * BLK]
    for part, tiles in enumerate((own0, own1)):
        row_block = half * 8 + res + 16 * (2 * step + part)
        rows = slice(part * BLK, (part + 1) * BLK)
        group = tab_ref[GROUP + half * 8 + 2 * step + part]

        @pl.when(group >= 0)
        def _():
            for source in range(8):
                col = tab_ref[COLUMN + half * 8 + source]
                at = pl.ds(pl.multiple_of(col * BLK, BLK), BLK)
                out_ref[rows, at] = out_ref[rows, at] + tiles[source]

        @pl.when(row_block < NPB)
        def _():
            out_ref[rows, :] = jnp.zeros((BLK, 16 * BLK), F32)

        @pl.when(front < NPB)
        def _():
            lane = pl.multiple_of(lax.min(front, NPB - 1) * BLK, BLK)
            row_id = lax.broadcasted_iota(jnp.int32, (BLK, BLK), 0) + row_block * BLK
            col_id = lax.broadcasted_iota(jnp.int32, (BLK, BLK), 1) + front * BLK
            out_ref[rows, :BLK] = jnp.where(row_id >= col_id, rows_ref[rows, pl.ds(lane, BLK)], 0.0)


def finish(tab, parent, arrived, rows, cols):
    def tiles(part):
        def pick(step, tab_ref):
            return (lax.max(tab_ref[GROUP + tab_ref[HALF] * 8 + 2 * step + part], 0), 0, 0)

        return pl.BlockSpec((8, BLK, BLK), pick)

    wide = [pl.BlockSpec((2 * NPIV, len(slots) * BLK), lambda step, tab_ref: (0, 0)) for slots in SLOTS]
    mine = lambda width: pl.BlockSpec((2 * BLK, width), lambda step, tab_ref: (step, 0))
    return pl.pallas_call(
        finish_kernel,
        out_shape=jax.ShapeDtypeStruct((8 * BLK, 16 * BLK), F32),
        grid_spec=pltpu.PrefetchScalarGridSpec(
            num_scalar_prefetch=1,
            grid=(4,),
            in_specs=[mine(16 * BLK), tiles(0), tiles(1), mine(NPIV)] + wide,
            out_specs=mine(16 * BLK),
        ),
        compiler_params=params(),
        name="finish",
    )(tab, parent, arrived, arrived, rows, *cols)


def enter_kernel(tab_ref, front_ref, tile_ref, out_ref):
    half, front = tab_ref[HALF], tab_ref[FRONT_AT]
    step = pl.program_id(0)
    count = tab_ref[CROSSINGS]

    @pl.when(step < lax.max(count, 1))
    def _():
        out_ref[...] = front_ref[...]

    row_block = half * 8 + tab_ref[RES] + 16 * tab_ref[CROSS + step]

    @pl.when((step < count) & (row_block >= NPB))
    def _():
        for source in range(8):
            col = tab_ref[COLUMN + (1 - half) * 8 + source]

            @pl.when(front + 8 * col >= NPB)
            def _():
                at = pl.ds(pl.multiple_of(col * BLK, BLK), BLK)
                out_ref[:, at] = out_ref[:, at] + tile_ref[source]


def enter(tab, front, crossed):
    row = pl.BlockSpec((BLK, 16 * BLK), lambda step, tab_ref: (tab_ref[CROSS + step], 0))

    def pick(step, tab_ref):
        return (lax.max(tab_ref[GROUP + (1 - tab_ref[HALF]) * 8 + tab_ref[CROSS + step]], 0), 0, 0)

    return pl.pallas_call(
        enter_kernel,
        out_shape=jax.ShapeDtypeStruct((8 * BLK, 16 * BLK), F32),
        grid_spec=pltpu.PrefetchScalarGridSpec(
            num_scalar_prefetch=1,
            grid=(8,),
            in_specs=[row, pl.BlockSpec((8, BLK, BLK), pick)],
            out_specs=row,
        ),
        input_output_aliases={1: 0},
        compiler_params=params(),
        name="enter",
    )(tab, front, crossed)


def shift(value, axis, size, away):
    return lax.ppermute(value, axis, [(i, (i + away) % size) for i in range(size)])


def gather_front(block, sources=4):
    near = [block]
    for away in range(1, 4):
        near.append(lax.ppermute(block, "x", [(i, (i + away) % 4) for i in range(sources)]))
    return near + [shift(piece, "core", 2, 1) for piece in near]


def row_routes():
    routes = []
    for c in range(16):
        for i in range(8):
            chip = (i // 2 + (c % 8) // 2) % 4
            routes.append((c + 16 * i, c * 8 + chip * 2 + i % 2))
    return routes


def staged(parent_front, child_entries, child_index):
    half, front = lax.axis_index("zh"), lax.axis_index("x") * 2 + lax.axis_index("core")
    pos = jnp.stack([half, lax.axis_index("zl") * 4 + lax.axis_index("y"), front]).astype(jnp.int32)
    tab = make_table(pos, child_index)
    packed = pack_tiles(tab, child_entries)
    arrived = lax.all_to_all(packed, ("zl", "y", "x", "core"), split_axis=0, concat_axis=0, tiled=True)

    strip = make_strip(tab, parent_front, arrived)
    pieces = lax.all_to_all(strip, CUBE, split_axis=0, concat_axis=0, tiled=True)
    summed = pieces[:NPB] + pieces[8:8 + NPB]
    one_block = summed[:, 0].reshape(NPIV, BLK)
    lead_cols = summed[:, 1].reshape(NPIV, BLK)

    along_z = [shift(one_block, ("zh", "zl"), 4, away) for away in range(1, 4)]
    lead_pieces = gather_front(lead_cols, 3)
    moved = lax.ppermute(one_block, CUBE + FRONT, row_routes())
    along_y = [one_block] + [shift(one_block, "y", 4, away) for away in range(1, 4)]
    along_z = jnp.stack(along_z)
    deep = [along_z]
    for away in range(1, 4):
        deep.append(shift(along_z, "y", 4, away))
    row_pieces = gather_front(moved)
    crossed = shift(arrived, "zh", 2, 1)

    inverse = lead_inverse(tab, lead_pieces)
    cols = [col_panel(inverse, along_y + [deep[0]])]
    cols.append(col_panel(inverse, [deep[1], deep[3]]))
    cols.append(col_panel(inverse, [deep[2]]))
    rows = row_panel(tab, inverse, row_pieces)
    schur = finish(tab, parent_front, arrived, rows, cols)
    return enter(tab, schur, crossed)


def solution(mesh):
    split = Mesh(mesh.devices.reshape(2, 2, 4, 4, 2), CUBE + FRONT)
    placed = P(CUBE, FRONT)
    return jax.shard_map(
        staged, mesh=split, in_specs=(placed, placed, P()), out_specs=placed, check_vma=False
    )
```
